32 devices in a mesh: replica: 8 (over z, x), fsdp: 4 (over y, core).
Axes of the slice: x: 2, y: 2, z: 4, core: 2. Of those that a mesh axis runs over, the one named last changes fastest.
Arguments:
- base: float32 [8192, 1024], P('fsdp'), may hold values from -6 to 6
- local: bfloat16 [8, 8192, 1024], P('replica', 'fsdp'), may hold values from -6 to 6
- momentum: float32 [8192, 1024], P('fsdp'), may hold values from -6 to 6
- tokens: bfloat16 [8, 2048, 8192], P('replica', 'fsdp'), may hold values from -6 to 6
- mask_embed: bfloat16 [8192], replicated, may hold values from -6 to 6
- mask_pos: int32 [8, 1, 768], P('replica'), may hold values from 0 to 2047, as said below
- cotangent: bfloat16 [8, 2048, 1024], P('replica', 'fsdp'), may hold values from -6 to 6
Outputs:
- new_momentum: bfloat16 [8192, 1024], P('fsdp')
- stepped: bfloat16 [8, 8192, 1024], P('replica', 'fsdp')
The draws below stay inside these ranges and needn't reach their ends.
Inputs may be any that keep to these rules, and one draw needn't show every extreme that they name: `mask_pos`: each row holds 768 different positions of its sequence.
All inputs are finite; a program needn't handle non-finite values. Where the reference program divides by a largest or mean magnitude, that divisor is 1e-20 or more.
Results may differ from the reference program's by a relative error of at most 0.008.
Values may be sent and summed in bfloat16 or wider, within the bound.
No kernel may reach another device: no remote copies, remote signals or barrier semaphores. Data moves between devices by JAX's collectives and lax.ppermute only.
A program may use at most 128 MiB of HBM per device.

```python
import jax
import jax.numpy as jnp
from jax import lax

D = 8192
KVW = 1024
QBLOCK = 128
LENGTH = 2048
NMASK = 768
SEQS = 1
TOKENS_R = 2048
N_REPLICA = 8
N_FSDP = 4


def draw_mask_pos(key, part):
    scores = jax.random.randint(key, (N_REPLICA, SEQS, LENGTH), 0, LENGTH, dtype=jnp.int32)
    scores = scores * LENGTH + jnp.arange(LENGTH, dtype=jnp.int32)[None, None, :]
    order = jnp.argsort(scores, axis=-1, stable=True)
    return order[:, :, :NMASK].astype(jnp.int32)


def block_scale(own_key, extent, split, least, top_value):
    def one(dim, parts):
        draws = jax.random.uniform(jax.random.fold_in(jax.random.fold_in(own_key, 6), dim), (parts,), jnp.float32, least / len(split), top_value / len(split))
        return jnp.repeat(jnp.exp(draws), extent[dim] // parts).reshape((-1,) + (1,) * (len(extent) - dim - 1))

    factor_of = one(*split[0])
    for cut in split[1:]:
        factor_of = factor_of * one(*cut)
    return factor_of


def normal_values(key, extent, spread, reach, cuts=(), held_as=jnp.bfloat16):
    factor_of = block_scale(key, extent, cuts, -0.22, 0.18) if cuts else 1.0
    entries = jax.random.normal(key, extent, jnp.float32) * spread * factor_of
    return jnp.minimum(jnp.maximum(entries, -reach), reach).astype(held_as)


def setup_inputs(seed: int = 0) -> dict:
    keys = jax.random.split(jax.random.key(seed), 8)
    return {
        "base": normal_values(keys[0], (D, KVW), 1.0, 6.0, ((0, 4),), jnp.float32),
        "local": normal_values(keys[1], (N_REPLICA, D, KVW), 1.0, 6.0, ((0, 8), (1, 4))),
        "momentum": normal_values(keys[2], (D, KVW), 1.0, 6.0, ((0, 4),), jnp.float32),
        "tokens": normal_values(keys[3], (N_REPLICA, TOKENS_R, D), 1.0, 6.0, ((0, 8), (1, 4))),
        "mask_embed": normal_values(keys[4], (D,), 1.0, 6.0),
        "mask_pos": draw_mask_pos(jax.random.fold_in(keys[7], 71), 0),
        "cotangent": normal_values(keys[6], (N_REPLICA, TOKENS_R, KVW), 1.0, 6.0, ((0, 8), (1, 4))),
    }


momentum_decay = 0.9
outer_rate = 0.7
inner_rate = 0.5


def dequantize(base, replica_params):
    drift = base - replica_params.astype(jnp.float32)
    blocks = drift.reshape(D, KVW // QBLOCK, QBLOCK)
    scales = (jnp.max(jnp.abs(blocks), axis=2, keepdims=True) + 1e-6).astype(jnp.bfloat16)
    code_vals = (blocks / scales.astype(jnp.float32)).astype(jnp.bfloat16)
    return (code_vals.astype(jnp.float32) * scales.astype(jnp.float32)).reshape(D, KVW)


def reference(base, local, momentum, tokens, mask_embed, mask_pos, cotangent):
    def add_replica(total, replica_params):
        return total + dequantize(base, replica_params), None

    summed, _ = lax.scan(add_replica, jnp.zeros((D, KVW), jnp.float32), local)
    outer_grad = summed / N_REPLICA
    momentum_next = momentum_decay * momentum + outer_grad
    renewed = base - outer_rate * (outer_grad + momentum_decay * momentum_next)

    def inner_step(triple):
        tok_block, positions, upstream = triple
        seq_index = jnp.arange(SEQS, dtype=jnp.int32)[:, None]
        marks = jnp.zeros((SEQS, LENGTH), jnp.int32).at[seq_index, positions].set(1).reshape(-1)
        inputs = jnp.where(marks[:, None] > 0, mask_embed[None, :], tok_block)
        group_in = inputs.reshape(N_FSDP, -1, D)
        group_up = upstream.reshape(N_FSDP, -1, KVW)

        def add_group(total, pair):
            term = lax.dot_general(pair[0], pair[1], (((0,), (0,)), ((), ())), preferred_element_type=jnp.float32)
            rounded = lax.optimization_barrier(term.astype(jnp.bfloat16))
            return total + rounded.astype(jnp.float32), None

        grad_sum, _ = lax.scan(add_group, jnp.zeros((D, KVW), jnp.float32), (group_in, group_up))
        gradient = grad_sum * (D ** -0.5)
        return (renewed - inner_rate * gradient).astype(jnp.bfloat16)

    stepped = lax.map(inner_step, (tokens, mask_pos, cotangent))
    return momentum_next.astype(jnp.bfloat16), stepped
```

```python
import functools

import jax
import jax.numpy as jnp
from jax import lax
from jax.experimental import pallas as pl
from jax.experimental.pallas import tpu as pltpu
from jax.sharding import PartitionSpec as P

D = 8192
QBLOCK = 128
LENGTH = 2048
LANES = 128
CHUNKS = 4

momentum_decay = 0.9
outer_rate = 0.7
inner_rate = 0.5

f32 = jnp.float32
bf16 = jnp.bfloat16


def call(kernel, grid, ins, outs, out_shape, name, flops=0, moved=0, aliases=None):
    return pl.pallas_call(
        kernel,
        grid_spec=pltpu.PrefetchScalarGridSpec(
            num_scalar_prefetch=1, grid=grid, in_specs=ins, out_specs=outs
        ),
        out_shape=out_shape,
        name=name,
        input_output_aliases=aliases or {},
        compiler_params=pltpu.CompilerParams(
            dimension_semantics=("arbitrary",) * len(grid)
        ),
        cost_estimate=pl.CostEstimate(
            flops=flops, bytes_accessed=moved, transcendentals=0
        ),
    )


def dequant(base, local):
    parts = []
    for q in range(base.shape[1] // QBLOCK):
        cols = slice(q * QBLOCK, (q + 1) * QBLOCK)
        drift = base[:, cols] - local[:, cols].astype(f32)
        peak = jnp.max(jnp.abs(drift), axis=1, keepdims=True)
        scale = (peak + 1e-06).astype(bf16).astype(f32)
        code = (drift / scale).astype(bf16).astype(f32)
        parts.append(code * scale)
    return jnp.concatenate(parts, axis=1)


def send_kernel(meta, base, local, out):
    out[...] = dequant(base, local).astype(bf16)


def pair_kernel(meta, base, local, got, out, keep):
    total = dequant(base, local) + got[...].astype(f32)
    step = pl.program_id(0)

    @pl.when(step < 2)
    def _():
        out[...] = total.astype(bf16)

    @pl.when(step >= 2)
    def _():
        keep[...] = total


def mask_kernel(tok_rows, meta, places, out):
    core = meta[2]
    for k in range(2):
        start = (meta[3] * 2 + (core if k == 0 else 1 - core)) * tok_rows
        place = start + lax.broadcasted_iota(jnp.int32, (tok_rows, 1), 0)
        hit = jnp.zeros((tok_rows, 1), f32)
        for s in range(places.shape[0]):
            same = place == places[s : s + 1, :] + s * LENGTH
            hit = jnp.maximum(
                hit, jnp.max(jnp.where(same, 1.0, 0.0), axis=1, keepdims=True)
            )
        out[k] = jnp.broadcast_to(hit, (tok_rows, LANES)).astype(bf16)


def masked(tok, mask, embed):
    parts = []
    for q in range(tok.shape[1] // LANES):
        cols = slice(q * LANES, (q + 1) * LANES)
        e = jnp.broadcast_to(embed[:, cols], (tok.shape[0], LANES))
        parts.append(jnp.where(mask > 0, e, tok[:, cols]))
    return jnp.concatenate(parts, axis=1)


def term(tok, cot):
    dims = (((0,), (0,)), ((), ()))
    return lax.dot_general(tok, cot, dims, preferred_element_type=f32).astype(bf16)


def grad_kernel(meta, mine, theirs, mask, embed, cot_mine, cot_theirs, out):
    a = term(masked(mine, mask[0], embed), cot_mine[...])
    b = term(masked(theirs, mask[1], embed), cot_theirs[...])
    out[...] = (a.astype(f32) + b.astype(f32)).astype(bf16)


def last_kernel(replicas, n_sent, meta, base, mom, own, *refs):
    sent, refs = refs[:n_sent], refs[n_sent:]
    g = refs[:4]
    new_mom, stepped = refs[-2:]
    step = pl.program_id(0)
    grad = own[...].astype(f32)
    for s in sent:
        grad = grad + s[...].astype(f32)
    grad = grad * D ** (-0.5)
    for k in range(4):

        @pl.when(step == k)
        def _(k=k):
            outer = g[k][...].astype(f32) / replicas
            nxt = momentum_decay * mom[...] + outer
            new_mom[...] = nxt.astype(bf16)
            renewed = base[...] - outer_rate * (outer + momentum_decay * nxt)
            stepped[...] = (renewed - inner_rate * grad).astype(bf16)


def flip(size, bit):
    return [(i, i ^ bit) for i in range(size)]


def body(base, local, momentum, tokens, mask_embed, mask_pos, cotangent):
    replicas, shards = lax.axis_size("replica"), lax.axis_size("fsdp")
    r, f = lax.axis_index("replica"), lax.axis_index("fsdp")
    rows, width = base.shape
    tok_rows = tokens.shape[1]
    local, tokens, cot = local[0], tokens[0], cotangent[0]
    embed = mask_embed[None, :]
    spot = jnp.arange(8, dtype=jnp.int32)
    meta = jnp.where(
        spot == 0,
        r & 1,
        jnp.where(spot == 1, (r >> 1) & 1, jnp.where(spot == 2, f & 1, f >> 1)),
    ).astype(jnp.int32)
    n = CHUNKS
    chunk = rows // n
    half, quarter = chunk // 2, chunk // 4
    highs = shards // 2
    shape = jax.ShapeDtypeStruct

    cot_theirs = lax.ppermute(cot, "fsdp", flip(shards, 1))

    def theirs(high, k, parts):
        size = rows // parts
        start = (high * 2 + 1 - (f & 1)) * rows + k * size
        cut = lax.dynamic_slice(tokens, (0, start), (tok_rows, size))
        return lax.ppermute(cut, "fsdp", flip(shards, 1))

    far = {
        (s, k): theirs((f >> 1) ^ s, k, n) for k in range(n) for s in range(1, highs)
    }
    near = theirs(f >> 1, 0, 1)

    tile = min(half, 128)
    per = half // tile
    sends = []
    for j in range(n):
        spec = pl.BlockSpec(
            (tile, width), lambda i, m, j=j: ((2 * j + 1 - m[0]) * per + i, 0)
        )
        sends.append(
            call(
                send_kernel,
                (per,),
                [spec, spec],
                pl.BlockSpec((tile, width), lambda i, m: (i, 0)),
                shape((half, width), bf16),
                "send",
                flops=20 * half * width,
                moved=8 * half * width,
            )(meta, base, local)
        )
    got_x = [lax.ppermute(s, "replica", flip(replicas, 1)) for s in sends]

    mask = call(
        functools.partial(mask_kernel, tok_rows),
        (1,),
        [pl.BlockSpec(mask_pos.shape[1:], lambda i, m: (0, 0))],
        pl.BlockSpec((2, tok_rows, LANES), lambda i, m: (0, 0, 0)),
        shape((2, tok_rows, LANES), bf16),
        "mask",
        flops=2 * tok_rows * mask_pos.shape[2],
        moved=4 * tok_rows * LANES,
    )(meta, mask_pos[0])

    def gradient(s, k, parts, other):
        size = rows // parts
        wide = min(size, 256)
        per = size // wide
        block = lambda i, m: (
            0,
            (((m[3] ^ s) * 2 + m[2]) * parts + k) * per + i,
        )
        whole = lambda i, m: (0, 0)
        return call(
            grad_kernel,
            (per,),
            [
                pl.BlockSpec((tok_rows, wide), block),
                pl.BlockSpec((tok_rows, wide), lambda i, m: (0, i)),
                pl.BlockSpec((2, tok_rows, LANES), lambda i, m: (0, 0, 0)),
                pl.BlockSpec((1, wide), block),
                pl.BlockSpec((tok_rows, width), whole),
                pl.BlockSpec((tok_rows, width), whole),
            ],
            pl.BlockSpec((wide, width), lambda i, m: (i, 0)),
            shape((size, width), bf16),
            "gradient",
            flops=4 * tok_rows * size * width,
            moved=4 * tok_rows * (size + width) + 2 * size * width,
        )(meta, tokens, other, mask, embed, cot, cot_theirs)

    sent = {}
    for k in range(n):
        for s in range(1, highs):
            part = gradient(s, k, n, far[s, k])
            sent[s, k] = lax.ppermute(part, "fsdp", flip(shards, 2 * s))
    own = gradient(0, 0, 1, near)

    small = quarter // 2
    sums = []
    for j in range(n):

        def block(i, m, j=j):
            g = jnp.where(i < 2, 1 - m[1], m[1])
            return ((2 * j + m[0]) * 4 + g * 2 + i % 2, 0)

        def got_block(i, m):
            g = jnp.where(i < 2, 1 - m[1], m[1])
            return (g * 2 + i % 2, 0)

        out, keep = call(
            pair_kernel,
            (4,),
            [
                pl.BlockSpec((small, width), block),
                pl.BlockSpec((small, width), block),
                pl.BlockSpec((small, width), got_block),
            ],
            [
                pl.BlockSpec((small, width), lambda i, m: (jnp.minimum(i, 1), 0)),
                pl.BlockSpec((small, width), lambda i, m: (jnp.maximum(i - 2, 0), 0)),
            ],
            [shape((quarter, width), bf16), shape((quarter, width), f32)],
            "pair",
            flops=20 * half * width,
            moved=9 * half * width,
        )(meta, base, local, got_x[j])
        got = lax.ppermute(out, "replica", flip(replicas, 2))
        total = (keep + got.astype(f32)).astype(bf16)
        bit = 4
        while bit < replicas:
            other = lax.ppermute(total, "replica", flip(replicas, bit))
            total = (total.astype(f32) + other.astype(f32)).astype(bf16)
            bit *= 2
        sums.append(
            [total]
            + [lax.ppermute(total, "replica", flip(replicas, b)) for b in (1, 2, 3)]
        )

    outs = []
    for j in range(n):
        place = lambda i, m, j=j: (
            4 * j + (m[0] ^ (i & 1)) * 2 + (m[1] ^ (i >> 1)),
            0,
        )
        inside = lambda i, m: ((m[0] ^ (i & 1)) * 2 + (m[1] ^ (i >> 1)), 0)
        spec = pl.BlockSpec((quarter, width), place)
        whole = pl.BlockSpec((quarter, width), lambda i, m: (0, 0))
        here = [sent[s, j] for s in range(1, highs)]
        n_in = 4 + len(here) + 4
        outs = call(
            functools.partial(last_kernel, replicas, len(here)),
            (4,),
            [spec] * 3
            + [pl.BlockSpec((quarter, width), inside)] * len(here)
            + [whole] * 4
            + [pl.BlockSpec(memory_space=pl.ANY)] * len(outs),
            [spec, spec],
            [shape((rows, width), bf16)] * 2,
            "last",
            flops=10 * chunk * width,
            moved=18 * chunk * width,
            aliases={n_in: 0, n_in + 1: 1} if outs else None,
        )(meta, base, momentum, own, *here, *sums[j], *outs)
    return outs[0], outs[1][None]


def solution(mesh):
    in_specs = (
        P("fsdp", None),
        P("replica", "fsdp", None),
        P("fsdp", None),
        P("replica", "fsdp", None),
        P(),
        P("replica", None, None),
        P("replica", "fsdp", None),
    )
    out_specs = (P("fsdp", None), P("replica", "fsdp", None))
    return jax.shard_map(
        body, mesh=mesh, in_specs=in_specs, out_specs=out_specs, check_vma=False
    )
```
